256 devices in a mesh: dp: 32 (over y, x, core), fsdp: 8 (over z).
Axes of the slice: x: 4, y: 4, z: 8, core: 2. Of those that a mesh axis runs over, the one named last changes fastest.
Arguments:
- queries: bfloat16 [12288, 3584], P('dp', 'fsdp'), may hold values from -52 to 52
- keys: bfloat16 [12288, 3584], P('dp', 'fsdp'), may hold values from -6 to 6
- values: bfloat16 [12288, 3584], P('dp', 'fsdp'), may hold values from -6 to 6
- out_grad: bfloat16 [12288, 7168], P('dp', 'fsdp'), may hold values from -6 to 6
- out_proj: bfloat16 [7168, 3584], P('dp', 'fsdp'), may hold values from -0.09375 to 0.09375
- doc_blocks: int32 [32, 3], replicated, may hold values from 1 to 4, as said below
- doc_device: int32 [32, 3], replicated, may hold values from 0 to 31, as said below
- doc_offset: int32 [32, 3], replicated, may hold values from 0 to 8, as said below
Outputs:
- query_grad: bfloat16 [24576, 3584], P('dp', 'fsdp')
- key_grad: bfloat16 [24576, 3584], P('dp', 'fsdp')
- value_grad: bfloat16 [24576, 3584], P('dp', 'fsdp')
- proj_grad: float32 [7168, 3584], P('dp', 'fsdp')
The draws below stay inside these ranges and needn't reach their ends.
Inputs may be any that keep to these rules, and one draw needn't show every extreme that they name: `doc_blocks`: every dp index holds 3 documents whose lengths add up to 6 blocks. `doc_device`: index s sends exactly one document to index (s + 1) mod 32 and exactly one to index (s - 1) mod 32, and computes its other documents itself. `doc_offset`: in the packed layout of an index, the document from the index before it starts at block 0, its own documents follow in their home order, then the document from the index after it; runs are disjoint, and some index fills all 12 blocks.
All inputs are finite; a program needn't handle non-finite values.
Results may differ from the reference program's by a relative error of at most 0.014.
Values may be sent and summed in bfloat16 or wider, within the bound.
No kernel may reach another device: no remote copies, remote signals or barrier semaphores. Data moves between devices by JAX's collectives and lax.ppermute only.
A program may use at most 128 MiB of HBM per device.

```python
import math
import jax
import jax.numpy as jnp
from jax import lax

D = 7168
HD = 112
HEADS = 32
BLK = 64
MOST = 4
HOME = 6
DOCUMENTS_PER_DP = 3
CAP = 12
TOKENS = 12288
PACKED = 24576
N_DP = 32


def packing(key):
    length_key = jax.random.fold_in(key, 11)
    right_key = jax.random.fold_in(key, 12)
    left_key = jax.random.fold_in(key, 13)
    pattern = jnp.tile(jnp.array([1, 1, MOST], jnp.int32), DOCUMENTS_PER_DP // 3)

    def ordering(sub_key):
        return jax.random.permutation(sub_key, DOCUMENTS_PER_DP).astype(jnp.int32)
    lengths = pattern[jax.vmap(ordering)(jax.random.split(length_key, N_DP))]
    right_neighbours = jax.vmap(ordering)(jax.random.split(right_key, N_DP))
    left_neighbours = jax.vmap(ordering)(jax.random.split(left_key, N_DP))
    sources = jnp.arange(N_DP, dtype=jnp.int32)[:, None]
    doc_ids = jnp.arange(DOCUMENTS_PER_DP, dtype=jnp.int32)[None, :]
    is_single = lengths == 1
    is_largest = lengths == MOST
    first_entry = sources == 0
    second_entry = sources == 1
    last_entry = sources == N_DP - 1
    right_extra = DOCUMENTS_PER_DP * (first_entry & is_single | last_entry & is_largest).astype(jnp.int32) - DOCUMENTS_PER_DP * (second_entry & is_largest).astype(jnp.int32)
    right_selection = lax.top_k(right_neighbours + right_extra, 1)[1][:, 0]
    is_rightward = doc_ids == right_selection[:, None]
    left_extra = DOCUMENTS_PER_DP * (first_entry & is_single | second_entry & is_largest).astype(jnp.int32) - 4 * DOCUMENTS_PER_DP * is_rightward.astype(jnp.int32)
    left_selection = lax.top_k(left_neighbours + left_extra, 1)[1][:, 0]
    is_left = doc_ids == left_selection[:, None]
    targets = jnp.where(is_rightward, (sources + 1) % N_DP, jnp.where(is_left, (sources + N_DP - 1) % N_DP, sources))
    right_len = jnp.sum(jnp.where(is_rightward, lengths, 0), axis=1)
    kept_len = jnp.where(is_rightward | is_left, 0, lengths)
    kept_start = jnp.cumsum(kept_len, axis=1) - kept_len
    kept_total = jnp.sum(kept_len, axis=1)
    left_offset = jnp.roll(right_len, 2) + jnp.roll(kept_total, 1)
    offsets = jnp.where(is_rightward, 0, jnp.where(is_left, left_offset[:, None], jnp.roll(right_len, 1)[:, None] + kept_start))
    return (lengths.astype(jnp.int32), targets.astype(jnp.int32), offsets.astype(jnp.int32))


def query_key(key):
    shape = (TOKENS, HEADS * HD)
    query_seed = jax.random.fold_in(key, 21)
    key_seed = jax.random.fold_in(key, 22)
    keys = jnp.clip(jax.random.normal(key_seed, shape, jnp.float32), -6.0, 6.0)
    queries = jnp.clip(jax.random.normal(query_seed, shape, jnp.float32), -6.0, 6.0)
    return (queries, keys)


def draw_queries(key, part):
    return query_key(key)[0].astype(jnp.bfloat16)


def draw_keys(key, part):
    return query_key(key)[1].astype(jnp.bfloat16)


def draw_doc_blocks(key, part):
    return packing(key)[0]


def draw_doc_device(key, part):
    return packing(key)[1]


def draw_doc_offset(key, part):
    return packing(key)[2]


def raised(values, own_key, source, target, blocks, factor):
    def block_of(axis_at):
        return (jnp.arange(values.shape[axis_at]) // (values.shape[axis_at] // blocks)).reshape((-1,) + (1,) * (values.ndim - 1 - axis_at))

    one_side = jax.random.permutation(own_key, blocks)[block_of(target)]
    second = (block_of(target) + blocks // 2) % blocks
    return jnp.where((block_of(source) == one_side) | (block_of(source) == second), factor * values, values)


def levels(own_key, dims, pieces, smallest, high):
    factor_of = 1.0
    for dim, shards_of in pieces:
        steps = jax.random.uniform(jax.random.fold_in(jax.random.fold_in(own_key, 6), dim), (shards_of,), jnp.float32, smallest / len(pieces), high / len(pieces))
        factor_of = factor_of * jnp.repeat(jnp.exp(steps), dims[dim] // shards_of).reshape((-1,) + (1,) * (len(dims) - 1 - dim))
    return factor_of


def bell_draw(own_key, extent, deviation, most, pieces=(), kind=jnp.bfloat16):
    values = jax.random.normal(own_key, extent, jnp.float32) * deviation
    if len(pieces) > 0:
        values = levels(own_key, extent, pieces, -0.22, 0.18) * values
    return jnp.clip(values, min=-most, max=most).astype(kind)


def bell_draw_with(key, extent, spread, limit, cuts, heavy, kind=jnp.bfloat16):
    values = spread * jax.random.normal(key, extent, jnp.float32)
    if cuts:
        values = values * levels(key, extent, cuts, -0.22, 0.18)
    return jnp.clip(raised(values, jax.random.fold_in(key, 3), *heavy), -limit, limit).astype(kind)


def setup_inputs(seed: int = 0) -> dict:
    key_list = jax.random.split(jax.random.key(seed), 9)
    return {
        "queries": draw_queries(jax.random.fold_in(key_list[8], 71), 0),
        "keys": draw_keys(jax.random.fold_in(key_list[8], 71), 0),
        "values": bell_draw(key_list[2], (TOKENS, HEADS * HD), 1.0, 6.0, ((0, 32), (1, 8))),
        "out_grad": bell_draw_with(key_list[3], (TOKENS, D), 1.0, 6.0, ((0, 32), (1, 8)), (0, 1, 32, 2.75)),
        "out_proj": bell_draw(key_list[4], (D, HEADS * HD), (HEADS * HD) ** -0.5, 0.09375, ((0, 32), (1, 8))),
        "doc_blocks": draw_doc_blocks(jax.random.fold_in(key_list[8], 71), 0),
        "doc_device": draw_doc_device(jax.random.fold_in(key_list[8], 71), 0),
        "doc_offset": draw_doc_offset(jax.random.fold_in(key_list[8], 71), 0),
    }


def attention(query_part, key_part, value_part, grad_part, doc_rows, position, slopes, valid_rows):
    score_scale = 1.0 / math.sqrt(query_part.shape[2])
    offsets = position.astype(jnp.float32)
    scores = jnp.einsum('qhd,khd->hqk', query_part.astype(jnp.float32), key_part.astype(jnp.float32)) * score_scale
    scores = scores - slopes[:, None, None] * (offsets[None, :, None] - offsets[None, None, :])
    allowed = (doc_rows[:, None] == doc_rows[None, :]) & (position[None, :] <= position[:, None])
    scores = jnp.where(allowed[None], scores, -1e+30)
    highest = lax.optimization_barrier(jnp.max(scores, axis=2, keepdims=True))
    weights_raw = jnp.exp(scores - highest)
    probabilities = weights_raw / lax.optimization_barrier(jnp.sum(weights_raw, axis=2, keepdims=True))
    prob_low = probabilities.astype(jnp.bfloat16)
    context = jnp.einsum('hqk,khd->qhd', prob_low.astype(jnp.float32), value_part.astype(jnp.float32)).astype(jnp.bfloat16)
    dprobs = jnp.einsum('qhd,khd->hqk', grad_part.astype(jnp.float32), value_part.astype(jnp.float32))
    row_delta = lax.optimization_barrier(jnp.sum(probabilities * dprobs, axis=2, keepdims=True))
    dscores = (probabilities * (dprobs - row_delta) * score_scale).astype(jnp.bfloat16)
    query_grad = jnp.einsum('hqk,khd->qhd', dscores.astype(jnp.float32), key_part.astype(jnp.float32)).astype(jnp.bfloat16)
    key_grad = jnp.einsum('hqk,qhd->khd', dscores.astype(jnp.float32), query_part.astype(jnp.float32)).astype(jnp.bfloat16)
    value_grad = jnp.einsum('hqk,qhd->khd', prob_low.astype(jnp.float32), grad_part.astype(jnp.float32)).astype(jnp.bfloat16)
    keep_rows = valid_rows[:, None, None]
    zero_value = jnp.zeros((), jnp.bfloat16)
    return (context, jnp.where(keep_rows, query_grad, zero_value), jnp.where(keep_rows, key_grad, zero_value), jnp.where(keep_rows, value_grad, zero_value))

def reference(queries, keys, values, out_grad, out_proj, doc_blocks, doc_device, doc_offset):
    width = HEADS * HD
    ctx_grad = jnp.dot(out_grad, out_proj, preferred_element_type=jnp.float32).astype(jnp.bfloat16)
    slopes = jnp.exp2(-(jnp.arange(HEADS, dtype=jnp.float32) + 1.0) / 4.0)
    starts_all = jnp.cumsum(doc_blocks, axis=1) - doc_blocks
    window = MOST * BLK
    inner = jnp.arange(window, dtype=jnp.int32)

    def one_device(source):
        token_index = ((source * HOME + starts_all[source]) * BLK)[:, None] + inner[None, :]
        valid_tokens = inner[None, :] < (doc_blocks[source] * BLK)[:, None]
        safe_index = jnp.where(valid_tokens, token_index, 0).astype(jnp.int32)

        def pick(table):
            rows_taken = jnp.where(valid_tokens[:, :, None], table[safe_index], jnp.zeros((), table.dtype))
            return rows_taken.reshape(DOCUMENTS_PER_DP, window, HEADS, HD)
        doc_rows = jnp.where(valid_tokens, 0, -1).astype(jnp.int32)

        def one_doc(query_part, key_part, value_part, grad_part, doc_mark):
            return attention(query_part, key_part, value_part, grad_part, doc_mark, inner, slopes, doc_mark >= 0)
        return jax.vmap(one_doc)(pick(queries), pick(keys), pick(values), pick(ctx_grad), doc_rows)
    context, q_home, k_home, v_home = lax.map(one_device, jnp.arange(N_DP, dtype=jnp.int32))
    device_ids = jnp.arange(N_DP, dtype=jnp.int32)[:, None]
    token_all = ((device_ids * HOME + starts_all) * BLK)[:, :, None] + inner[None, None, :]
    valid_all = inner[None, None, :] < (doc_blocks * BLK)[:, :, None]
    home_index = jnp.where(valid_all, token_all, TOKENS).astype(jnp.int32).reshape(-1)
    home_context = jnp.zeros((TOKENS, width), jnp.bfloat16).at[home_index].set(context.reshape(-1, width), mode='drop')
    packed_index = jnp.where(valid_all, ((doc_device * CAP + doc_offset) * BLK)[:, :, None] + inner[None, None, :], PACKED)
    packed_index = packed_index.astype(jnp.int32).reshape(-1)

    def place(result):
        return jnp.zeros((PACKED, width), jnp.bfloat16).at[packed_index].set(result.reshape(-1, width), mode='drop')
    grad_scale = 1.0 / math.sqrt(TOKENS)
    grad_rows = out_grad.reshape(N_DP, HOME * BLK, D)
    context_rows = home_context.reshape(N_DP, HOME * BLK, width)

    def add_partial(running, pair):
        partial_sum = lax.dot_general(pair[0], pair[1], (((0,), (0,)), ((), ())), preferred_element_type=jnp.float32) * grad_scale
        rounded = lax.optimization_barrier(partial_sum.astype(jnp.bfloat16))
        return (running + rounded.astype(jnp.float32), None)
    proj_grad, _ = lax.scan(add_partial, jnp.zeros((D, width), jnp.float32), (grad_rows, context_rows))
    return (place(q_home), place(k_home), place(v_home), proj_grad)
```

```python
import functools
import math

import jax
import jax.numpy as jnp
from jax import lax
from jax.experimental import pallas as pl
from jax.experimental.pallas import tpu as pltpu
from jax.sharding import PartitionSpec as P

HD = 112
BLK = 64
MOST = 4
TILE = 128
NX = 4
NZ = 8
STEPS = (0, -1, 1, -2, 2, -3, 3, 4)

SMEM = pl.BlockSpec(memory_space=pltpu.SMEM)
VMEM = pl.BlockSpec(memory_space=pltpu.VMEM)
ANY = pl.BlockSpec(memory_space=pl.ANY)
PARAMS = pltpu.CompilerParams(vmem_limit_bytes=56 * 1024 * 1024)


def dp_of(y, x, c):
    return (y % NX) * 2 * NX + (x % NX) * 2 + c


def first_axis(step):
    return [
        (dp_of(y, x, c), dp_of(y, x + step, c) if c == 0 else dp_of(y + step, x, c))
        for y in range(NX) for x in range(NX) for c in range(2)
    ]


def second_axis(step):
    return [
        (dp_of(y, x, c), dp_of(y + step, x, c) if c == 0 else dp_of(y, x + step, c))
        for y in range(NX) for x in range(NX) for c in range(2)
    ]


def core_swap():
    return [(i, i ^ 1) for i in range(2 * NX * NX)]


def ring(step):
    return [(i, (i + step) % NZ) for i in range(NZ)]


def dot(a, b, dims):
    return lax.dot_general(a, b, (dims, ((), ())), preferred_element_type=jnp.float32)


def coords(place):
    my = place[0]
    return my >> 3, (my >> 1) & 3, my & 1, place[1]


def slot_of(y, x, c, py, px):
    dy = (py - y) & 3
    dx = (px - x) & 3
    return jnp.where(c == 0, dx * NX + dy, dy * NX + dx)


def forward_kernel(place, doc_blocks, q, k, v, context, probs):
    rows = q.shape[0]
    heads = q.shape[1] // HD
    scale = 1.0 / math.sqrt(HD)
    my = place[0]
    head0 = place[1] * heads
    bound1 = doc_blocks[my, 0] * BLK
    bound2 = bound1 + doc_blocks[my, 1] * BLK
    for r in range(rows // TILE):
        width = TILE * (r + 1)
        row = lax.broadcasted_iota(jnp.int32, (TILE, width), 0) + r * TILE
        col = lax.broadcasted_iota(jnp.int32, (TILE, width), 1)
        start = jnp.where(row >= bound2, bound2, jnp.where(row >= bound1, bound1, 0))
        allowed = (col <= row) & (col >= start)
        distance = (row - col).astype(jnp.float32)
        for h in range(heads):
            lanes = slice(h * HD, (h + 1) * HD)
            power = jnp.full((1, 1), head0 + (h + 1), jnp.int32).astype(jnp.float32)
            slope = jnp.exp2(power * -0.25)
            scores = dot(q[r * TILE : width, lanes], k[0:width, lanes], ((1,), (1,))) * scale
            scores = scores - slope * distance
            scores = jnp.where(allowed, scores, -1e30)
            highest = jnp.max(scores, axis=1, keepdims=True)
            raw = jnp.exp(scores - highest)
            prob = raw / jnp.sum(raw, axis=1, keepdims=True)
            probs[h, r * TILE : width, 0:width] = prob
            out = dot(prob.astype(jnp.bfloat16), v[0:width, lanes], ((1,), (0,)))
            context[r * TILE : width, lanes] = out.astype(jnp.bfloat16)


def forward(place, doc_blocks, q, k, v):
    rows, width = q.shape
    return pl.pallas_call(
        forward_kernel,
        out_shape=(
            jax.ShapeDtypeStruct((rows, width), jnp.bfloat16),
            jax.ShapeDtypeStruct((width // HD, rows, rows), jnp.float32),
        ),
        in_specs=[SMEM, SMEM, VMEM, VMEM, VMEM],
        out_specs=(VMEM, VMEM),
        compiler_params=PARAMS,
        name="attn_forward",
    )(place, doc_blocks, q, k, v)


def sent_start(place, doc_blocks, doc_device, shift, count):
    my = place[0]
    target = (my + shift) & (count - 1)
    start = jnp.int32(0)
    run = jnp.int32(0)
    for d in range(doc_blocks.shape[1]):
        start = jnp.where(doc_device[my, d] == target, run, start)
        run = run + doc_blocks[my, d]
    return start


def backward_kernel(place, doc_blocks, doc_device, q, k, v, g, probs,
                    dq, dk, dv, send_right, send_left, ds_all, low_all, padded):
    rows, width = q.shape
    heads = width // HD
    count = doc_blocks.shape[0]
    scale = 1.0 / math.sqrt(HD)
    tiles = rows // TILE
    for h in range(heads):
        lanes = slice(h * HD, (h + 1) * HD)
        for r in range(tiles):
            wide = TILE * (r + 1)
            band = slice(r * TILE, wide)
            prob = probs[h, band, 0:wide]
            dprob = dot(g[band, lanes], v[0:wide, lanes], ((1,), (1,)))
            delta = jnp.sum(prob * dprob, axis=1, keepdims=True)
            ds = (prob * (dprob - delta) * scale).astype(jnp.bfloat16)
            ds_all[band, 0:wide] = ds
            low_all[band, 0:wide] = prob.astype(jnp.bfloat16)
            padded[0, band, lanes] = dot(ds, k[0:wide, lanes], ((1,), (0,))).astype(jnp.bfloat16)
        for t in range(tiles):
            below = slice(t * TILE, rows)
            band = slice(t * TILE, (t + 1) * TILE)
            padded[1, band, lanes] = dot(
                ds_all[below, band], q[below, lanes], ((0,), (0,))
            ).astype(jnp.bfloat16)
            padded[2, band, lanes] = dot(
                low_all[below, band], g[below, lanes], ((0,), (0,))
            ).astype(jnp.bfloat16)
    for n, out in enumerate((dq, dk, dv)):
        out[...] = padded[n, 0:rows, :]
    for shift, send in ((1, send_right), (-1, send_left)):
        start = sent_start(place, doc_blocks, doc_device, shift, count)
        for n in range(3):
            for m in range(MOST):
                at = pl.multiple_of((start + m) * BLK, BLK)
                send[n, m * BLK : (m + 1) * BLK, :] = padded[n, pl.ds(at, BLK), :]


def backward(place, doc_blocks, doc_device, q, k, v, g, probs):
    rows, width = q.shape
    grad = jax.ShapeDtypeStruct((rows, width), jnp.bfloat16)
    moved = jax.ShapeDtypeStruct((3, MOST * BLK, width), jnp.bfloat16)
    return pl.pallas_call(
        backward_kernel,
        out_shape=(grad, grad, grad, moved, moved),
        in_specs=[SMEM, SMEM, SMEM] + [VMEM] * 5,
        out_specs=(VMEM,) * 5,
        scratch_shapes=[
            pltpu.VMEM((rows, rows), jnp.bfloat16),
            pltpu.VMEM((rows, rows), jnp.bfloat16),
            pltpu.VMEM((3, rows + MOST * BLK, width), jnp.bfloat16),
        ],
        compiler_params=PARAMS,
        name="attn_backward",
    )(place, doc_blocks, doc_device, q, k, v, g, probs)


def place_kernel(place, doc_blocks, doc_device, doc_offset, dq, dk, dv, from_left, from_right,
                 q_out, k_out, v_out, pool):
    rows, width = dq.shape
    count, docs = doc_blocks.shape
    home = rows // BLK
    my = place[0]
    zero_block = home + 2 * MOST
    for n, mine in enumerate((dq, dk, dv)):
        pool[n, 0:rows, :] = mine[...]
        pool[n, rows : rows + MOST * BLK, :] = from_left[n]
        pool[n, rows + MOST * BLK : rows + 2 * MOST * BLK, :] = from_right[n]
        pool[n, rows + 2 * MOST * BLK :, :] = jnp.zeros((BLK, width), jnp.bfloat16)
    runs = []
    first = jnp.int32(0)
    for d in range(docs):
        length = doc_blocks[my, d]
        live = doc_device[my, d] == my
        runs.append((doc_offset[my, d], jnp.where(live, length, 0), first))
        first = first + length
    for shift, base in ((-1, home), (1, home + MOST)):
        source = (my + shift) & (count - 1)
        for d in range(docs):
            live = doc_device[source, d] == my
            length = jnp.where(live, doc_blocks[source, d], 0)
            runs.append((doc_offset[source, d], length, jnp.int32(base)))
    for b in range(q_out.shape[0] // BLK):
        block = jnp.int32(zero_block)
        for offset, length, base in runs:
            inside = (b >= offset) & (b < offset + length)
            block = jnp.where(inside, base + b - offset, block)
        at = pl.multiple_of(block * BLK, BLK)
        for n, out in enumerate((q_out, k_out, v_out)):
            out[b * BLK : (b + 1) * BLK, :] = pool[n, pl.ds(at, BLK), :]


def to_packed(place, doc_blocks, doc_device, doc_offset, dq, dk, dv, from_left, from_right):
    rows, width = dq.shape
    packed = (rows // BLK - 2 + 2 * MOST) * BLK
    grad = jax.ShapeDtypeStruct((packed, width), jnp.bfloat16)
    return pl.pallas_call(
        place_kernel,
        out_shape=(grad, grad, grad),
        in_specs=[SMEM] * 4 + [VMEM] * 5,
        out_specs=(VMEM,) * 3,
        scratch_shapes=[pltpu.VMEM((3, rows + (2 * MOST + 1) * BLK, width), jnp.bfloat16)],
        compiler_params=PARAMS,
        name="to_packed",
    )(place, doc_blocks, doc_device, doc_offset, dq, dk, dv, from_left, from_right)


def partial_kernel(steps, pieces, scale, aliased, place, context, *refs):
    grads = refs[: sum(pieces)]
    rest = refs[sum(pieces) + (2 if aliased else 0) :]
    keep, send, stage, sems = rest
    y, x, c, z = coords(place)
    part = stage.shape[2]
    copies = []
    taken = 0
    for n, step in enumerate(steps):
        total = None
        row = 0
        for _ in range(pieces[n]):
            grad = grads[taken]
            taken += 1
            count = grad.shape[0]
            term = dot(grad[...], context[row : row + count, :], ((0,), (0,)))
            total = term if total is None else total + term
            row += count
        low = (total * scale).astype(jnp.bfloat16)
        far = (z + step) & (NZ - 1)
        for j in range(2):
            even = low[2 * j * part : (2 * j + 1) * part]
            odd = low[(2 * j + 1) * part : (2 * j + 2) * part]
            slot = n * 4 + j * 2
            stage[n, 2 * j] = jnp.where(c == 0, even, odd)
            stage[n, 2 * j + 1] = jnp.where(c == 0, odd, even)
            py = far >> 1
            px = ((far & 1) << 1) + j
            for m, (out, core) in enumerate(((keep, c), (send, 1 - c))):
                copy = pltpu.make_async_copy(
                    stage.at[n, 2 * j + m], out.at[slot_of(y, x, core, py, px)], sems.at[slot + m]
                )
                copy.start()
                copies.append(copy)
    for copy in copies:
        copy.wait()


def partials(steps, scale, place, context, grads, previous):
    pieces = tuple(len(g) for g in grads)
    flat = [g for group in grads for g in group]
    width = context.shape[1]
    features = flat[0].shape[1]
    part = features // 4
    half = jax.ShapeDtypeStruct((NX * NX, part, width), jnp.bfloat16)
    aliased = previous is not None
    extra = list(previous) if aliased else []
    first = 2 + len(flat)
    return pl.pallas_call(
        functools.partial(partial_kernel, steps, pieces, scale, aliased),
        out_shape=(half, half),
        in_specs=[SMEM] + [VMEM] * (1 + len(flat)) + [ANY] * len(extra),
        out_specs=(ANY, ANY),
        scratch_shapes=[
            pltpu.VMEM((len(steps), 4, part, width), jnp.bfloat16),
            pltpu.SemaphoreType.DMA((len(steps) * 4,)),
        ],
        input_output_aliases={first: 0, first + 1: 1} if aliased else {},
        compiler_params=PARAMS,
        name="proj_partial",
    )(place, context, *flat, *extra)


def cotangent_kernel(pieces, place, *refs):
    grads = refs[: sum(pieces)]
    own, other, out, weights, total, sems = refs[sum(pieces) :]
    y, x, c, z = coords(place)
    part = own.shape[1]
    copies = []
    for n, step in enumerate(STEPS):
        far = (z + step) & (NZ - 1)
        group = []
        for j in range(2):
            py = far >> 1
            px = ((far & 1) << 1) + j
            for m, (source, core) in enumerate(((own, c), (other, 1 - c))):
                at = pl.multiple_of((2 * j + core) * part, part)
                copy = pltpu.make_async_copy(
                    source.at[slot_of(y, x, core, py, px)],
                    weights.at[n, pl.ds(at, part)],
                    sems.at[n * 4 + j * 2 + m],
                )
                copy.start()
                group.append(copy)
        copies.append(group)
    taken = 0
    for n in range(len(STEPS)):
        for copy in copies[n]:
            copy.wait()
        row = 0
        for _ in range(pieces[n]):
            grad = grads[taken]
            taken += 1
            count = grad.shape[0]
            term = dot(grad[...], weights[n], ((1,), (0,)))
            if n == 0:
                total[row : row + count, :] = term
            else:
                total[row : row + count, :] += term
            row += count
    out[...] = total[...].astype(jnp.bfloat16)


def cotangent(place, grads, own, other):
    pieces = tuple(len(g) for g in grads)
    flat = [g for group in grads for g in group]
    rows = sum(g.shape[0] for g in grads[-1])
    part, width = own.shape[1:]
    return pl.pallas_call(
        functools.partial(cotangent_kernel, pieces),
        out_shape=jax.ShapeDtypeStruct((rows, width), jnp.bfloat16),
        in_specs=[SMEM] + [VMEM] * len(flat) + [ANY, ANY],
        out_specs=VMEM,
        scratch_shapes=[
            pltpu.VMEM((len(STEPS), 4 * part, width), jnp.bfloat16),
            pltpu.VMEM((rows, width), jnp.float32),
            pltpu.SemaphoreType.DMA((len(STEPS) * 4,)),
        ],
        compiler_params=PARAMS,
        name="cotangent",
    )(place, *flat, own, other)


def on_device(queries, keys, values, out_grad, out_proj, doc_blocks, doc_device, doc_offset):
    count = doc_blocks.shape[0]
    my_index = lax.axis_index("dp").astype(jnp.int32)
    my_z = lax.axis_index("fsdp").astype(jnp.int32)
    place = jnp.stack([my_index, my_z])
    rows = queries.shape[0]
    width = queries.shape[1]
    part = out_proj.shape[0]
    half = rows // 2

    def along(value, step):
        return lax.ppermute(value, "fsdp", ring(step))

    def over(value, pairs):
        return lax.ppermute(value, "dp", pairs)

    back1 = along(out_grad, 1)
    ahead1 = along(out_grad, -1)
    got = [out_proj] + [over(out_proj, first_axis(NX - s)) for s in range(1, NX)]
    context, probs = forward(place, doc_blocks, queries, keys, values)
    back2 = along(back1, 1)
    ahead2 = along(ahead1, -1)
    line = jnp.stack(got)
    lines = [line] + [over(line, second_axis(NX - s)) for s in range(1, NX)]
    own = jnp.stack(lines, axis=1).reshape(NX * NX, part, width)
    other = over(own, core_swap())
    back3 = along(back2, 1)
    ahead3 = along(ahead2, -1)
    far_low = along(back3[:half], 1)
    far_high = along(ahead3[half:], -1)

    grad_scale = 1.0 / math.sqrt(rows * count)
    done = partials(STEPS[:5], grad_scale, place, context,
                    [(out_grad,), (back1,), (ahead1,), (back2,), (ahead2,)], None)
    done = partials(STEPS[5:7], grad_scale, place, context, [(back3,), (ahead3,)], done)
    keep, send = partials(STEPS[7:], grad_scale, place, context, [(far_low, far_high)], done)

    shape4 = (NX, NX, part, width)
    keep = keep.reshape(shape4)
    came = over(send, core_swap()).reshape(shape4)

    def wide(value):
        return value.astype(jnp.float32)

    ctx_grad = cotangent(
        place,
        [(out_grad,), (back1,), (ahead1,), (back2,), (ahead2,), (back3,), (ahead3,),
         (far_low, far_high)],
        own, other)

    parts = [over((wide(keep[s]) + wide(came[s])).astype(jnp.bfloat16), first_axis(s))
             for s in range(1, NX)]
    dq, dk, dv, send_right, send_left = backward(
        place, doc_blocks, doc_device, queries, keys, values, ctx_grad, probs)
    line_sum = wide(keep[0]) + wide(came[0])
    for p in parts:
        line_sum = line_sum + wide(p)
    lasts = [over(line_sum[s].astype(jnp.bfloat16), second_axis(s)) for s in range(1, NX)]
    from_left = over(send_right, [(i, (i + 1) % count) for i in range(count)])
    from_right = over(send_left, [(i, (i - 1) % count) for i in range(count)])
    q_out, k_out, v_out = to_packed(
        place, doc_blocks, doc_device, doc_offset, dq, dk, dv, from_left, from_right)
    proj = line_sum[0]
    for p in lasts:
        proj = proj + wide(p)
    return q_out, k_out, v_out, proj


def solution(mesh):
    spec = P("dp", "fsdp")
    return jax.shard_map(
        on_device,
        mesh=mesh,
        in_specs=(spec,) * 5 + (P(), P(), P()),
        out_specs=(spec,) * 4,
        check_vma=False,
    )
```
